1024 devices in a mesh: dp: 4 (over z_hi), pipe: 16 (over x, z_lo), expert: 16 (over y, core).
Axes of the slice: x: 4, y: 8, z: 16 (z_hi: 4, z_lo: 4; z = z_hi * 4 + z_lo), core: 2. Of those that a mesh axis runs over, the one named last changes fastest.
Arguments:
- output_grads: bfloat16 [4, 16, 2048, 4096], P('dp', 'pipe', 'expert'), may hold values from -4 to 4
- gate_values: float32 [4, 16, 2048, 8], P('dp', 'pipe', 'expert'), may hold values from 0.1 to 1
- routing: int32 [4, 16, 2048, 8], P('dp', 'pipe', 'expert'), may hold values from 0 to 127, as said below
- saved_inputs: bfloat16 [4, 16, 1, 16, 16, 4096], P('dp', 'pipe'), may hold values from -6 to 6
- expert_weights: bfloat16 [16, 3, 1536, 4096], P('pipe', None, 'expert'), may hold values from -0.09375 to 0.09375
Outputs:
- passed_grads: bfloat16 [4, 16, 2048, 4096], P('dp', 'pipe', 'expert')
- weight_grads: bfloat16 [16, 3, 1536, 4096], P('pipe', None, 'expert', 'dp')
The draws below stay inside these ranges and needn't reach their ends.
Inputs may be any that keep to these rules, and one draw needn't show every extreme that they name: `routing`: each token names 8 different experts. Among the 128 tokens of one device (each aligned block of 128 tokens of a micro-batch), every expert below 1 is named by 1 to 16 tokens. In some replica and section, one such expert is named by exactly 16 tokens of every device of the expert axis.
All inputs are finite; a program needn't handle non-finite values.
Results may differ from the reference program's by a relative error of at most 0.014.
Values may be sent and summed in bfloat16 or wider, within the bound.
A program may use at most 32 MiB of HBM per device.

```python
import functools
import jax
import jax.numpy as jnp
from jax import lax

D = 4096
EXPERTS = 128
TOP = 8
HIDDEN_SIZE = 1536
TOK = 128
CAP = 16
EXP_FLIGHT = 1
SPLIT = 16
HID_DEV = 96
WIN_ROWS = 1536
TOKENS = 2048
N_DP = 4
N_PIPE = 16
N_EXPERT = 16


def draw_routing(key, part):
    groups = N_DP * N_PIPE
    blocks = groups * N_EXPERT
    subkeys = jax.random.split(key, 7)
    counts = jax.random.randint(subkeys[0], (blocks, EXP_FLIGHT), 1, CAP + 1)
    hottest = jnp.repeat(jax.random.randint(subkeys[1], (groups,), 0, EXP_FLIGHT), N_EXPERT)
    full_group = jax.random.randint(subkeys[5], (groups,), 0, 2)
    forced = jax.random.randint(subkeys[6], (), 0, groups)
    full_group = jnp.where(jnp.arange(groups) == forced, 1, full_group)
    full_block = jnp.repeat(full_group, N_EXPERT)
    expert_index = jnp.arange(EXP_FLIGHT)
    filled = (expert_index[None, :] == hottest[:, None]) & (full_block[:, None] == 1)
    counts = jnp.where(filled, CAP, counts)
    shuffle = jax.random.randint(subkeys[2], (blocks, EXP_FLIGHT, TOK), 0, 2 ** 20) * TOK + jnp.arange(TOK)
    ranking = jnp.argsort(jnp.argsort(shuffle, axis=-1), axis=-1)
    member = ranking < counts[:, :, None]
    window = jnp.transpose(member, (0, 2, 1))
    padded = jnp.concatenate([window, jnp.zeros((blocks, TOK, EXPERTS - EXP_FLIGHT), dtype=jnp.bool_)], axis=-1)
    columns = jnp.arange(EXPERTS)
    scores = jax.random.randint(subkeys[3], (blocks, TOK, EXPERTS), 0, 2 ** 20) * EXPERTS + columns
    scores = jnp.where(padded, 2 ** 30 + columns, jnp.where(columns < EXP_FLIGHT, -1, scores))
    top_scores, chosen = lax.top_k(scores, TOP)
    mixing = jax.random.randint(subkeys[4], (blocks, TOK, TOP), 0, 2 ** 20) * TOP + jnp.arange(TOP)
    column_order = jnp.argsort(mixing, axis=-1)
    chosen = jnp.take_along_axis(chosen, column_order, axis=-1)
    return chosen.reshape(N_DP, N_PIPE, N_EXPERT * TOK, TOP).astype(jnp.int32)


def shard_levels(rng, dims, pieces, low, largest):
    def one(axis_at, shards_of):
        draws = jax.random.uniform(jax.random.fold_in(jax.random.fold_in(rng, 6), axis_at), (shards_of,), jnp.float32, low / len(pieces), largest / len(pieces))
        return jnp.repeat(jnp.exp(draws), dims[axis_at] // shards_of).reshape((-1,) + (1,) * (len(dims) - axis_at - 1))

    level = one(*pieces[0])
    for cut in pieces[1:]:
        level = level * one(*cut)
    return level


def normal_values(stream_key, dims, spread, bound, cuts=(), kind=jnp.bfloat16):
    entries = spread * jax.random.normal(stream_key, dims, jnp.float32)
    if cuts:
        entries = entries * shard_levels(stream_key, dims, cuts, -0.22, 0.18)
    return jnp.clip(entries, -bound, bound).astype(kind)


def setup_inputs(seed: int = 0) -> dict:
    streams_of = jax.random.split(jax.random.key(seed), 6)
    output_grads = normal_values(streams_of[0], (N_DP, N_PIPE, TOKENS, D), 0.5, 4.0, ((0, 4), (1, 16), (2, 16)))
    gate_values = jnp.clip(0.1 + 0.9 * jax.random.uniform(streams_of[1], (N_DP, N_PIPE, TOKENS, TOP), jnp.float32) ** shard_levels(streams_of[1], (N_DP, N_PIPE, TOKENS, TOP), ((0, 4), (1, 16), (2, 16)), -0.2, 0.2), 0.1, 1.0)
    routing = draw_routing(jax.random.fold_in(streams_of[5], 71), 0)
    saved_inputs = normal_values(streams_of[3], (N_DP, N_PIPE, EXP_FLIGHT, N_EXPERT, CAP, D), 1.0, 6.0, ((0, 4), (1, 16)))
    expert_weights = normal_values(streams_of[4], (N_PIPE, 3, WIN_ROWS, D), D ** -0.5, 0.09375, ((0, 16), (2, 16)))
    return dict(output_grads=output_grads, gate_values=gate_values, routing=routing, saved_inputs=saved_inputs, expert_weights=expert_weights)


def route_tables(routing, gate_values, flight, capacity):
    expert_index = jnp.arange(flight, dtype=jnp.int32)
    matches = routing[:, :, None] == expert_index[None, None, :]
    member = jnp.any(matches, axis=1)
    gate_share = jnp.sum(jnp.where(matches, gate_values[:, :, None], jnp.float32(0.0)), axis=1)
    member_count = member.astype(jnp.int32)
    slot_index = jnp.cumsum(member_count, axis=0) - member_count
    chooser = (slot_index[None, :, :] == jnp.arange(capacity, dtype=jnp.int32)[:, None, None]) & member[None, :, :]
    selector = jnp.transpose(chooser, (2, 0, 1))
    return member, slot_index, gate_share, selector


def group_pass(section_grads, section_routing, section_gates, section_saved, weights_section):
    sources = section_grads.reshape(N_EXPERT, TOK, D)
    tables = jax.vmap(functools.partial(route_tables, flight=EXP_FLIGHT, capacity=CAP))
    member, slot_index, gate_share, selector = tables(section_routing.reshape(N_EXPERT, TOK, TOP), section_gates.reshape(N_EXPERT, TOK, TOP))
    picked = jnp.einsum('sect,std->secd', selector.astype(jnp.float32), sources.astype(jnp.float32), precision=lax.Precision.HIGHEST)
    weighting = jnp.sum(jnp.where(selector, jnp.transpose(gate_share, (0, 2, 1))[:, :, None, :], jnp.float32(0.0)), axis=-1)
    routed = (picked * weighting[:, :, :, None]).astype(jnp.bfloat16)
    summed_list = []
    grad_list = []
    by_rows = (((0,), (0,)), ((), ()))
    for expert in range(EXP_FLIGHT):
        own_inputs = section_saved[expert].reshape(N_EXPERT * CAP, D)
        routed_rows = routed[:, expert].reshape(N_EXPERT * CAP, D)
        base = expert * HIDDEN_SIZE
        gate_weight = weights_section[0, base:base + HIDDEN_SIZE]
        up_weight = weights_section[1, base:base + HIDDEN_SIZE]
        down_weight = weights_section[2, base:base + HIDDEN_SIZE]
        gate_pre = jnp.dot(own_inputs, gate_weight.T, preferred_element_type=jnp.float32)
        up_pre = jnp.dot(own_inputs, up_weight.T, preferred_element_type=jnp.float32)
        sigmoid_gate = jax.nn.sigmoid(gate_pre)
        activated = gate_pre * sigmoid_gate
        hidden = (activated * up_pre).astype(jnp.bfloat16)
        hidden_grad = jnp.dot(routed_rows, down_weight.T, preferred_element_type=jnp.float32)
        gate_grad = (hidden_grad * up_pre * sigmoid_gate * (1.0 + gate_pre * (1.0 - sigmoid_gate))).astype(jnp.bfloat16)
        up_grad = (hidden_grad * activated).astype(jnp.bfloat16)
        rows_count = N_EXPERT * CAP
        partial_gate = jnp.einsum('rsh,shd->rsd', gate_grad.reshape(rows_count, SPLIT, HID_DEV).astype(jnp.float32), gate_weight.reshape(SPLIT, HID_DEV, D).astype(jnp.float32), precision=lax.Precision.HIGHEST)
        partial_up = jnp.einsum('rsh,shd->rsd', up_grad.reshape(rows_count, SPLIT, HID_DEV).astype(jnp.float32), up_weight.reshape(SPLIT, HID_DEV, D).astype(jnp.float32), precision=lax.Precision.HIGHEST)
        partial_value = lax.optimization_barrier((partial_gate + partial_up).astype(jnp.bfloat16))
        summed = jnp.sum(partial_value.astype(jnp.float32), axis=1)
        summed_list.append(summed.reshape(N_EXPERT, CAP, D))
        grad_gate = lax.dot_general(gate_grad, own_inputs, by_rows, preferred_element_type=jnp.float32)
        grad_up = lax.dot_general(up_grad, own_inputs, by_rows, preferred_element_type=jnp.float32)
        grad_down = lax.dot_general(hidden, routed_rows, by_rows, preferred_element_type=jnp.float32)
        grad_list.append(jnp.stack([grad_gate, grad_up, grad_down]))
    summed_all = jnp.stack(summed_list, axis=1)
    source_index = jnp.arange(N_EXPERT, dtype=jnp.int32)[:, None, None]
    expert_index = jnp.arange(EXP_FLIGHT, dtype=jnp.int32)[None, None, :]
    clipped = jnp.minimum(slot_index, CAP - 1)
    gathered = summed_all[source_index, expert_index, clipped]
    added = jnp.sum(jnp.where(member[:, :, :, None], gathered, jnp.float32(0.0)), axis=2)
    input_grads = (sources.astype(jnp.float32) + added).astype(jnp.bfloat16).reshape(TOKENS, D)
    replica_grads = jnp.concatenate(grad_list, axis=1).astype(jnp.bfloat16)
    return input_grads, replica_grads


def reference(output_grads, gate_values, routing, saved_inputs, expert_weights):
    def per_section(section):
        weights_section = lax.dynamic_index_in_dim(expert_weights, section, 0, keepdims=False)
        total = jnp.zeros((3, WIN_ROWS, D), jnp.float32)
        results = []
        for replica in range(N_DP):
            section_grads = lax.dynamic_index_in_dim(output_grads[replica], section, 0, keepdims=False)
            section_gates = lax.dynamic_index_in_dim(gate_values[replica], section, 0, keepdims=False)
            section_routing = lax.dynamic_index_in_dim(routing[replica], section, 0, keepdims=False)
            section_saved = lax.dynamic_index_in_dim(saved_inputs[replica], section, 0, keepdims=False)
            input_grads, replica_grads = group_pass(section_grads, section_routing, section_gates, section_saved, weights_section)
            total = total + replica_grads.astype(jnp.float32)
            results.append(input_grads)
        return jnp.stack(results), total.astype(jnp.bfloat16)

    all_inputs, weight_grads = lax.map(per_section, jnp.arange(N_PIPE, dtype=jnp.int32))
    all_inputs = jnp.transpose(all_inputs, (1, 0, 2, 3))
    passed_grads = jnp.roll(all_inputs, -1, axis=1)
    return passed_grads, weight_grads
```

```python
import functools

import jax
import jax.numpy as jnp
from jax import lax
from jax.experimental import pallas as pl
from jax.experimental.pallas import tpu as pltpu
from jax.sharding import PartitionSpec as P

MESH = pl.DeviceIdType.MESH
BF16 = jnp.bfloat16
F32 = jnp.float32
NT = (((1,), (1,)), ((), ()))
TN = (((0,), (0,)), ((), ()))


def one_hot(routing, capacity):
    tokens = routing.shape[1]
    hit = routing == 0
    member = jnp.max(jnp.where(hit, F32(1.0), F32(0.0)), axis=0, keepdims=True)
    before = lax.broadcasted_iota(jnp.int32, (tokens, tokens), 0) < lax.broadcasted_iota(
        jnp.int32, (tokens, tokens), 1
    )
    upper = jnp.where(before, F32(1.0), F32(0.0)).astype(BF16)
    rows = jnp.broadcast_to(member, (capacity, tokens))
    slot = jnp.dot(rows.astype(BF16), upper, preferred_element_type=F32)
    index = lax.broadcasted_iota(jnp.int32, (capacity, tokens), 0).astype(F32)
    return hit, jnp.where((slot == index) & (rows > 0.5), F32(1.0), F32(0.0))


def kernel(
    n_y, n_dp, n_pipe,
    routing_ref, gates_ref, og_hbm, x_hbm, w_hbm,
    passed_ref, grads_ref,
    og, x, w_gu, w_d, rows_all, picked, slices, relay, acts, acts_in, both, wide, part,
    ring_in, ring_out, og_in, routing_in, final, final_in, acc_gu, acc_d, act_g, act_u,
    load_sem, og_send, og_recv, rt_send, rt_recv, fin_send, fin_recv, w_send, w_recv,
    y_send, y_recv, ysib_send, ysib_recv, s_send, s_recv, ssib_send, ssib_recv,
    xy_send, xy_recv, rl_send, rl_recv, rf_send, rf_recv,
    h_send, h_recv, hf_send, hf_recv, g_send, g_recv, gf_send, gf_recv,
    t_send, t_recv, r_send, r_recv,
):
    dp = lax.axis_index("dp")
    pipe = lax.axis_index("pipe")
    expert = lax.axis_index("expert")
    y = expert // 2
    core = expert % 2
    far = n_y // 2
    cap, width = rows_all.shape[1], rows_all.shape[2]
    half = width // 2
    hid = w_d.shape[0]
    tokens = og.shape[0]
    part_d = width // n_dp
    tile = width // 8
    sib = {"expert": y * 2 + (1 - core)}
    y_to = ({"expert": ((y + 1) % n_y) * 2 + core}, {"expert": ((y + n_y - 1) % n_y) * 2 + core})
    d_to = ({"dp": (dp + 1) % n_dp}, {"dp": (dp + n_dp - 1) % n_dp})
    p_to = {"pipe": (pipe + n_pipe - 1) % n_pipe}
    p_from = {"pipe": (pipe + 1) % n_pipe}

    sent = []

    def send(src, dst, ssem, rsem, to):
        copy = pltpu.make_async_remote_copy(
            src_ref=src, dst_ref=dst, send_sem=ssem, recv_sem=rsem, device_id=to,
            device_id_type=MESH,
        )
        copy.start()
        sent.append(copy)

    def arrived(dst, rsem, to):
        pltpu.make_async_remote_copy(
            src_ref=dst, dst_ref=dst, send_sem=rsem, recv_sem=rsem, device_id=to,
            device_id_type=MESH,
        ).wait_recv()

    loads = [
        pltpu.make_async_copy(og_hbm, og, load_sem.at[0]),
        pltpu.make_async_copy(x_hbm, x, load_sem.at[1]),
        pltpu.make_async_copy(w_hbm.at[pl.ds(0, 2)], w_gu.at[core], load_sem.at[2]),
        pltpu.make_async_copy(w_hbm.at[2], w_d, load_sem.at[3]),
    ]
    barrier = pltpu.get_barrier_semaphore()
    peers = (sib, *y_to, *d_to, p_to, p_from)
    for peer in peers:
        pl.semaphore_signal(barrier, inc=1, device_id=peer, device_id_type=MESH)
    for load in loads:
        load.start()

    hit, chooser = one_hot(routing_ref[...], cap)
    share = jnp.sum(jnp.where(hit, gates_ref[...], F32(0.0)), axis=0, keepdims=True)
    weighting = jnp.sum(chooser * share, axis=1, keepdims=True)
    chooser = chooser.astype(BF16)
    loads[0].wait()
    for at in range(4):
        cols = pl.ds(at * (width // 4), width // 4)
        chosen = jnp.dot(chooser, og[:, cols], preferred_element_type=F32)
        picked[:, cols] = chosen
        rows_all[expert, :, cols] = (chosen * weighting).astype(BF16)
    pl.semaphore_wait(barrier, len(peers))

    def gather(piece, ring_send, ring_recv, sib_send, sib_recv):
        def owner(offset):
            return ((y + offset + n_y) % n_y) * 2 + core

        def first():
            for d, order in ((0, (0, 1)), (1, (1, 0))):
                for h in order:
                    send(piece(expert, h), piece(expert, h), ring_send.at[d, 0, h],
                         ring_recv.at[d, 0, h], y_to[d])
            for h in (0, 1):
                send(piece(expert, h), piece(expert, h), sib_send.at[0, h], sib_recv.at[0, h], sib)

        def step(k):
            for at in (0, 1):
                for d in (0, 1):
                    h = at if d == 0 else 1 - at
                    if k == far and at == 1:
                        continue
                    offset = -k if d == 0 else k
                    block = piece(owner(offset), h)
                    arrived(block, ring_recv.at[d, k - 1, h], y_to[d])
                    if k < far - 1 or (k == far - 1 and at == 0):
                        send(block, block, ring_send.at[d, k, h], ring_recv.at[d, k, h], y_to[d])
                    slot = offset % n_y
                    send(block, block, sib_send.at[slot, h], sib_recv.at[slot, h], sib)

        def finish():
            for offset in range(n_y):
                for h in (0, 1):
                    other = ((y + offset) % n_y) * 2 + (1 - core)
                    arrived(piece(other, h), sib_recv.at[offset, h], sib)

        return first, step, finish

    ag_first, ag_step, ag_finish = gather(
        lambda e, h: rows_all.at[e, :, pl.ds(h * half, half)], y_send, y_recv, ysib_send, ysib_recv
    )
    sl_first, sl_step, sl_finish = gather(
        lambda e, h: slices.at[e, pl.ds(3 * h, 3)], s_send, s_recv, ssib_send, ssib_recv
    )

    def send_slices(src, kind):
        for d in (0, 1):
            peer = (dp + 1) % n_dp if d == 0 else (dp + n_dp - 1) % n_dp
            near = pl.ds(pl.multiple_of(peer * part_d, part_d), part_d)
            send(src.at[expert, :, near], slices.at[expert, 3 * kind + d],
                 xy_send.at[kind, d], xy_recv.at[kind, d], d_to[d])
            base = ((dp + 2) % n_dp) * part_d + d * (part_d // 2)
            beyond = pl.ds(pl.multiple_of(base, part_d // 2), part_d // 2)
            send(src.at[expert, :, beyond], relay.at[d, kind],
                 rl_send.at[kind, d], rl_recv.at[kind, d], d_to[d])

    def relay_slices(kind):
        for d in (0, 1):
            arrived(relay.at[d, kind], rl_recv.at[kind, d], d_to[d])
            send(relay.at[d, kind],
                 slices.at[expert, 3 * kind + 2, :, pl.ds(d * (part_d // 2), part_d // 2)],
                 rf_send.at[kind, d], rf_recv.at[kind, d], d_to[d])

    def slices_arrived(kind):
        for d in (0, 1):
            arrived(slices.at[expert, 3 * kind + d], xy_recv.at[kind, d], d_to[d])
            arrived(slices.at[expert, 3 * kind + 2, :, pl.ds(d * (part_d // 2), part_d // 2)],
                    rf_recv.at[kind, d], d_to[d])

    og_rows = tokens // 4

    def send_og(at):
        block = pl.ds(at * og_rows, og_rows)
        send(og_hbm.at[block], og_in.at[block], og_send.at[at], og_recv.at[at], p_to)

    ag_first()
    send_slices(x_hbm, 0)
    send_slices(rows_all, 1)
    send(routing_ref, routing_in, rt_send, rt_recv, p_to)
    send(w_hbm.at[pl.ds(0, 2)], w_gu.at[core], w_send, w_recv, sib)
    send_og(0)

    loads[1].wait()
    loads[2].wait()

    def into(weights, rows_ref, out_rows):
        def body(at, total):
            cols = pl.ds(pl.multiple_of(at * tile, tile), tile)
            rows = rows_ref[:, :, cols].reshape(-1, tile)
            return total + lax.dot_general(weights(cols), rows, NT, preferred_element_type=F32)
        rows = rows_ref.shape[0] * rows_ref.shape[1]
        return lax.fori_loop(0, width // tile, body, jnp.zeros((out_rows, rows), F32))

    pre = into(lambda cols: w_gu[core, :, :, cols].reshape(2 * hid, tile), x, 2 * hid)
    gate_pre, up_pre = pre[:hid], pre[hid:]
    sigmoid = jax.nn.sigmoid(gate_pre)
    activated = gate_pre * sigmoid
    acts[0:hid, :] = (activated * up_pre).astype(BF16)
    act_g[...] = up_pre * sigmoid * (1.0 + gate_pre * (1.0 - sigmoid))
    act_u[...] = activated
    hidden_rows = pl.ds(0, hid)
    for d in (0, 1):
        send(acts.at[hidden_rows], acts_in.at[d, hidden_rows], h_send.at[d], h_recv.at[d], d_to[d])
    send_og(1)
    send_og(2)

    def relay_hidden():
        for d in (0, 1):
            arrived(acts_in.at[d, hidden_rows], h_recv.at[d], d_to[d])
            rows = pl.ds(d * (hid // 2), hid // 2)
            send(acts_in.at[d, rows], acts_in.at[2, rows], hf_send.at[d], hf_recv.at[d], d_to[d])

    for k in range(1, far):
        ag_step(k)
        if k == 1:
            relay_slices(0)
            relay_slices(1)
    slices_arrived(0)
    slices_arrived(1)
    sl_first()
    relay_hidden()
    ag_step(far)
    ag_finish()

    loads[3].wait()
    hidden_grad = into(lambda cols: w_d[:, cols], rows_all, hid)
    gate_grad = (hidden_grad * act_g[...]).astype(BF16)
    up_grad = (hidden_grad * act_u[...]).astype(BF16)
    acts[hid:2 * hid, :] = gate_grad
    acts[2 * hid:3 * hid, :] = up_grad
    both[core, 0:hid, :] = gate_grad
    both[core, hid:2 * hid, :] = up_grad
    send(acts.at[pl.ds(hid, 2 * hid)], both.at[core], t_send, t_recv, sib)
    for at in (0, 1):
        for d in (0, 1):
            m = at if d == 0 else 1 - at
            rows = pl.ds((1 + m) * hid, hid)
            send(acts.at[rows], acts_in.at[d, rows], g_send.at[d, m], g_recv.at[d, m], d_to[d])
    send_og(3)

    def relay_grads():
        for d in (0, 1):
            rows = pl.ds((1 + d) * hid, hid)
            arrived(acts_in.at[d, rows], g_recv.at[d, d], d_to[d])
            send(acts_in.at[d, rows], acts_in.at[2, rows], gf_send.at[d], gf_recv.at[d], d_to[d])

    arrived(both.at[1 - core], t_recv, sib)
    arrived(w_gu.at[1 - core], w_recv, sib)
    turned = jnp.transpose(both[...].reshape(4 * hid, rows_all.shape[0] * cap).astype(F32))
    wide[...] = turned.reshape(n_y, 2, cap, 4 * hid)
    mine = wide[:, core].reshape(n_y * cap, 4 * hid).astype(BF16)

    def partials(h):
        def body(at, carry):
            cols = pl.ds(pl.multiple_of(h * half + at * tile, tile), tile)
            weights = w_gu[:, :, :, cols].reshape(4 * hid, tile)
            part[:, :, cols] = jnp.dot(mine, weights, preferred_element_type=F32).reshape(
                n_y, cap, tile
            )
            return carry
        lax.fori_loop(0, half // tile, body, 0)

    def rs_send(d, k, h):
        cols = pl.ds(h * half, half)
        dest = (y + (k if d == 0 else -k) + n_y) % n_y
        value = part[dest, :, cols]
        if k < far and not (k == far - 1 and h != d):
            arrived(ring_in.at[d, k, :, cols], r_recv.at[d, k, h], y_to[d])
            value = value + ring_in[d, k, :, cols].astype(F32)
        ring_out[d, k - 1, :, cols] = value.astype(BF16)
        send(ring_out.at[d, k - 1, :, cols], ring_in.at[d, k - 1, :, cols],
             r_send.at[d, k - 1, h], r_recv.at[d, k - 1, h], y_to[d])

    def rs_step(k):
        for at in (1, 0) if k == far - 1 else (0, 1):
            for d in (0, 1):
                rs_send(d, k, at if d == 0 else 1 - at)

    def add_grads(j, gate_up, down):
        own = j is None
        base = pl.multiple_of(dp * part_d, part_d)
        cell = part_d // 2
        for at in (0, 1):
            cols = pl.ds(at * cell, cell)
            here = pl.ds(pl.multiple_of(base + at * cell, cell), cell)
            if gate_up:
                left = acts[hid:3 * hid, :] if own else acts_in[j, hid:3 * hid, :]
                right = x[:, :, here] if own else slices[:, j, :, cols]
                value = jnp.dot(left, right.reshape(-1, cell), preferred_element_type=F32)
                acc_gu[:, cols] = value if own else acc_gu[:, cols] + value
            if down:
                left = acts[0:hid, :] if own else acts_in[j, 0:hid, :]
                right = rows_all[:, :, here] if own else slices[:, 3 + j, :, cols]
                value = jnp.dot(left, right.reshape(-1, cell), preferred_element_type=F32)
                acc_d[:, cols] = value if own else acc_d[:, cols] + value

    partials(0)
    rs_send(0, far, 0)
    partials(1)
    rs_send(1, far, 1)
    sl_step(1)
    for k in range(far - 1, 0, -1):
        rs_step(k)
        if k == far - 1:
            add_grads(None, True, True)
        if k == far - 2 or far < 3:
            relay_grads()
        if far - k + 1 <= far:
            sl_step(far - k + 1)

    for h in (0, 1):
        cols = pl.ds(h * half, half)
        for d in (0, 1):
            if far > 1 or h == d:
                arrived(ring_in.at[d, 0, :, cols], r_recv.at[d, 0, h], y_to[d])
        total = part[y, :, cols] + (ring_in[0, 0, :, cols].astype(F32) + ring_in[1, 0, :, cols].astype(F32))
        final[:, cols] = (picked[:, cols] + total).astype(BF16)
        send(final.at[:, cols], final_in.at[:, cols], fin_send.at[h], fin_recv.at[h], p_to)

    sl_finish()
    for d in (0, 1):
        rows = pl.ds(d * (hid // 2), hid // 2)
        arrived(acts_in.at[2, rows], hf_recv.at[d], d_to[d])
    for j in range(3):
        add_grads(j, False, True)
    for d in (0, 1):
        rows = pl.ds((2 - d) * hid, hid)
        arrived(acts_in.at[d, rows], g_recv.at[d, 1 - d], d_to[d])
        add_grads(d, True, False)

    arrived(routing_in, rt_recv, p_to)
    _, placed = one_hot(routing_in[...], cap)
    placed = placed.astype(BF16)
    named = lax.dot_general(
        placed, jnp.ones((cap, 128), BF16), TN, preferred_element_type=F32
    )[:, 0:1] > 0.5
    for at in range(4):
        block = pl.ds(at * og_rows, og_rows)
        arrived(og_in.at[block], og_recv.at[at], p_to)
    for h in (0, 1):
        arrived(final_in.at[:, pl.ds(h * half, half)], fin_recv.at[h], p_to)
    for at in range(4):
        cols = pl.ds(at * (width // 4), width // 4)
        value = lax.dot_general(placed, final_in[:, cols], TN, preferred_element_type=F32)
        passed_ref[:, cols] = jnp.where(named, value, og_in[:, cols].astype(F32)).astype(BF16)

    for d in (0, 1):
        rows = pl.ds((1 + d) * hid, hid)
        arrived(acts_in.at[2, rows], gf_recv.at[d], d_to[d])
    add_grads(2, True, False)
    grads_ref[0] = acc_gu[0:hid, :].astype(BF16)
    grads_ref[1] = acc_gu[hid:2 * hid, :].astype(BF16)
    grads_ref[2] = acc_d[...].astype(BF16)
    for copy in sent:
        copy.wait_send()


def shards(output_grads, gate_values, routing, saved_inputs, expert_weights):
    n_dp, n_pipe = lax.axis_size("dp"), lax.axis_size("pipe")
    devices = lax.axis_size("expert")
    n_y = devices // 2
    far = n_y // 2
    cap, width = saved_inputs.shape[4], saved_inputs.shape[5]
    tokens = output_grads.shape[2]
    hid = expert_weights.shape[2]
    rows = devices * cap
    part_d = width // n_dp
    DMA = pltpu.SemaphoreType.DMA
    V = pltpu.VMEM
    scratch = [
        V((tokens, width), BF16),
        V((devices, cap, width), BF16),
        V((2, 2, hid, width), BF16),
        V((hid, width), BF16),
        V((devices, cap, width), BF16),
        V((cap, width), F32),
        V((devices, 6, cap, part_d), BF16),
        V((2, 2, cap, part_d // 2), BF16),
        V((3 * hid, rows), BF16),
        V((3, 3 * hid, rows), BF16),
        V((2, 2 * hid, rows), BF16),
        V((n_y, 2, cap, 4 * hid), F32),
        V((n_y, cap, width), F32),
        V((2, far, cap, width), BF16),
        V((2, far, cap, width), BF16),
        V((tokens, width), BF16),
        V(routing.shape[:1:-1], jnp.int32),
        V((cap, width), BF16),
        V((cap, width), BF16),
        V((2 * hid, part_d), F32),
        V((hid, part_d), F32),
        V((hid, rows), F32),
        V((hid, rows), F32),
        DMA((4,)), DMA((4,)), DMA((4,)), DMA, DMA, DMA((2,)), DMA((2,)), DMA, DMA,
        DMA((2, far, 2)), DMA((2, far, 2)), DMA((n_y, 2)), DMA((n_y, 2)),
        DMA((2, far, 2)), DMA((2, far, 2)), DMA((n_y, 2)), DMA((n_y, 2)),
        DMA((2, 2)), DMA((2, 2)), DMA((2, 2)), DMA((2, 2)), DMA((2, 2)), DMA((2, 2)),
        DMA((2,)), DMA((2,)), DMA((2,)), DMA((2,)), DMA((2, 2)), DMA((2, 2)), DMA((2,)), DMA((2,)),
        DMA, DMA, DMA((2, far, 2)), DMA((2, far, 2)),
    ]
    vmem = pl.BlockSpec(memory_space=pltpu.VMEM)
    anywhere = pl.BlockSpec(memory_space=pl.ANY)
    passed, grads = pl.pallas_call(
        functools.partial(kernel, n_y, n_dp, n_pipe),
        out_shape=(
            jax.ShapeDtypeStruct((tokens, width), BF16),
            jax.ShapeDtypeStruct((3, hid, part_d), BF16),
        ),
        in_specs=[vmem, vmem, anywhere, anywhere, anywhere],
        out_specs=(vmem, vmem),
        scratch_shapes=scratch,
        compiler_params=pltpu.CompilerParams(
            collective_id=0, has_side_effects=True, vmem_limit_bytes=48 << 20
        ),
        name="expert_backward",
    )(
        jnp.transpose(routing[0, 0]),
        jnp.transpose(gate_values[0, 0]),
        output_grads[0, 0],
        saved_inputs[0, 0, 0],
        expert_weights[0],
    )
    return passed[None, None], grads[None]


def solution(mesh):
    placed = (
        P("dp", "pipe", "expert", None),
        P("dp", "pipe", "expert", None),
        P("dp", "pipe", "expert", None),
        P("dp", "pipe", None, None, None, None),
        P("pipe", None, "expert", None),
    )
    return jax.shard_map(
        shards,
        mesh=mesh,
        in_specs=placed,
        out_specs=(P("dp", "pipe", "expert", None), P("pipe", None, "expert", "dp")),
        check_vma=False,
    )
```

```python
import functools

import jax
import jax.numpy as jnp
from jax import lax
from jax.experimental import pallas as pl
from jax.experimental.pallas import tpu as pltpu
from jax.sharding import PartitionSpec as P

MESH = pl.DeviceIdType.MESH
BF16 = jnp.bfloat16
F32 = jnp.float32
NT = (((1,), (1,)), ((), ()))
TN = (((0,), (0,)), ((), ()))


def one_hot(routing, capacity):
    tokens = routing.shape[1]
    hit = routing == 0
    member = jnp.max(jnp.where(hit, F32(1.0), F32(0.0)), axis=0, keepdims=True)
    before = lax.broadcasted_iota(jnp.int32, (tokens, tokens), 0) < lax.broadcasted_iota(
        jnp.int32, (tokens, tokens), 1
    )
    upper = jnp.where(before, F32(1.0), F32(0.0)).astype(BF16)
    rows = jnp.broadcast_to(member, (capacity, tokens))
    slot = jnp.dot(rows.astype(BF16), upper, preferred_element_type=F32)
    index = lax.broadcasted_iota(jnp.int32, (capacity, tokens), 0).astype(F32)
    return hit, jnp.where((slot == index) & (rows > 0.5), F32(1.0), F32(0.0))


def kernel(
    n_y, n_dp, n_pipe,
    routing_hbm, gates_hbm, og_hbm, x_hbm, w_hbm,
    passed_ref, grads_ref,
    routing_ref, gates_ref, og, x, w_gu, w_d, rows_all, picked, slices, relay, acts, acts_in, both, wide, part,
    ring_in, ring_out, og_in, routing_in, final, final_in, acc_gu, acc_d, act_g, act_u,
    load_sem, og_send, og_recv, rt_send, rt_recv, fin_send, fin_recv, w_send, w_recv,
    y_send, y_recv, ysib_send, ysib_recv, s_send, s_recv, ssib_send, ssib_recv,
    xy_send, xy_recv, rl_send, rl_recv, rf_send, rf_recv,
    h_send, h_recv, hf_send, hf_recv, g_send, g_recv, gf_send, gf_recv,
    t_send, t_recv, r_send, r_recv,
):
    dp = lax.axis_index("dp")
    pipe = lax.axis_index("pipe")
    expert = lax.axis_index("expert")
    y = expert // 2
    core = expert % 2
    far = n_y // 2
    cap, width = rows_all.shape[1], rows_all.shape[2]
    half = width // 2
    hid = w_d.shape[0]
    tokens = og.shape[0]
    part_d = width // n_dp
    tile = width // 8
    sib = {"expert": y * 2 + (1 - core)}
    y_to = ({"expert": ((y + 1) % n_y) * 2 + core}, {"expert": ((y + n_y - 1) % n_y) * 2 + core})
    d_to = ({"dp": (dp + 1) % n_dp}, {"dp": (dp + n_dp - 1) % n_dp})
    p_to = {"pipe": (pipe + n_pipe - 1) % n_pipe}
    p_from = {"pipe": (pipe + 1) % n_pipe}

    sent = []

    def send(src, dst, ssem, rsem, to):
        copy = pltpu.make_async_remote_copy(
            src_ref=src, dst_ref=dst, send_sem=ssem, recv_sem=rsem, device_id=to,
            device_id_type=MESH,
        )
        copy.start()
        sent.append(copy)

    def arrived(dst, rsem, to):
        pltpu.make_async_remote_copy(
            src_ref=dst, dst_ref=dst, send_sem=rsem, recv_sem=rsem, device_id=to,
            device_id_type=MESH,
        ).wait_recv()

    loads = [
        pltpu.make_async_copy(og_hbm, og, load_sem.at[0]),
        pltpu.make_async_copy(x_hbm, x, load_sem.at[1]),
        pltpu.make_async_copy(w_hbm.at[pl.ds(0, 2)], w_gu.at[core], load_sem.at[2]),
        pltpu.make_async_copy(w_hbm.at[2], w_d, load_sem.at[3]),
        pltpu.make_async_copy(routing_hbm, routing_ref, load_sem.at[4]),
        pltpu.make_async_copy(gates_hbm, gates_ref, load_sem.at[5]),
    ]
    barrier = pltpu.get_barrier_semaphore()
    peers = (sib, *y_to, *d_to, p_from)
    for peer in peers:
        pl.semaphore_signal(barrier, inc=1, device_id=peer, device_id_type=MESH)
    for at in (4, 5, 0, 1, 2, 3):
        loads[at].start()

    loads[4].wait()
    loads[5].wait()
    hit, chooser = one_hot(routing_ref[...], cap)
    share = jnp.sum(jnp.where(hit, gates_ref[...], F32(0.0)), axis=0, keepdims=True)
    weighting = jnp.sum(chooser * share, axis=1, keepdims=True)
    chooser = chooser.astype(BF16)
    loads[0].wait()
    for at in range(4):
        cols = pl.ds(at * (width // 4), width // 4)
        chosen = jnp.dot(chooser, og[:, cols], preferred_element_type=F32)
        picked[:, cols] = chosen
        rows_all[expert, :, cols] = (chosen * weighting).astype(BF16)
    loads[1].wait()
    loads[2].wait()

    def into(weights, rows_ref, out_rows):
        def body(at, total):
            cols = pl.ds(pl.multiple_of(at * tile, tile), tile)
            rows = rows_ref[:, :, cols].reshape(-1, tile)
            return total + lax.dot_general(weights(cols), rows, NT, preferred_element_type=F32)
        rows = rows_ref.shape[0] * rows_ref.shape[1]
        return lax.fori_loop(0, width // tile, body, jnp.zeros((out_rows, rows), F32))

    pre = into(lambda cols: w_gu[core, :, :, cols].reshape(2 * hid, tile), x, 2 * hid)
    pl.semaphore_wait(barrier, len(peers))

    def gather(piece, ring_send, ring_recv, sib_send, sib_recv):
        def owner(offset):
            return ((y + offset + n_y) % n_y) * 2 + core

        def first(pieces=(0, 1)):
            for at in range(len(pieces)):
                for d in (0, 1):
                    h = pieces[at if d == 0 else len(pieces) - 1 - at]
                    send(piece(expert, h), piece(expert, h), ring_send.at[d, 0, h],
                         ring_recv.at[d, 0, h], y_to[d])
            for h in pieces:
                send(piece(expert, h), piece(expert, h), sib_send.at[0, h], sib_recv.at[0, h], sib)

        def step(k, pieces=(0, 1)):
            for at in range(len(pieces)):
                for d in (0, 1):
                    h = pieces[at if d == 0 else len(pieces) - 1 - at]
                    if k == far and h != d:
                        continue
                    offset = -k if d == 0 else k
                    block = piece(owner(offset), h)
                    arrived(block, ring_recv.at[d, k - 1, h], y_to[d])
                    if k < far - 1 or (k == far - 1 and h == d):
                        send(block, block, ring_send.at[d, k, h], ring_recv.at[d, k, h], y_to[d])
                    slot = offset % n_y
                    send(block, block, sib_send.at[slot, h], sib_recv.at[slot, h], sib)

        def finish():
            for offset in range(n_y):
                for h in (0, 1):
                    other = ((y + offset) % n_y) * 2 + (1 - core)
                    arrived(piece(other, h), sib_recv.at[offset, h], sib)

        return first, step, finish

    ag_first, ag_step, ag_finish = gather(
        lambda e, h: rows_all.at[e, :, pl.ds(h * half, half)], y_send, y_recv, ysib_send, ysib_recv
    )
    sl_first, sl_step, sl_finish = gather(
        lambda e, h: slices.at[e, pl.ds(3 * h, 3)], s_send, s_recv, ssib_send, ssib_recv
    )

    def send_slices(src, kind):
        for d in (0, 1):
            peer = (dp + 1) % n_dp if d == 0 else (dp + n_dp - 1) % n_dp
            near = pl.ds(pl.multiple_of(peer * part_d, part_d), part_d)
            base = ((dp + 2) % n_dp) * part_d + d * (part_d // 2)
            beyond = pl.ds(pl.multiple_of(base, part_d // 2), part_d // 2)
            send(src.at[expert, :, beyond], relay.at[d, kind],
                 rl_send.at[kind, d], rl_recv.at[kind, d], d_to[d])
            send(src.at[expert, :, near], slices.at[expert, 3 * kind + d],
                 xy_send.at[kind, d], xy_recv.at[kind, d], d_to[d])

    def relay_slices(kind):
        for d in (0, 1):
            arrived(relay.at[d, kind], rl_recv.at[kind, d], d_to[d])
            send(relay.at[d, kind],
                 slices.at[expert, 3 * kind + 2, :, pl.ds(d * (part_d // 2), part_d // 2)],
                 rf_send.at[kind, d], rf_recv.at[kind, d], d_to[d])

    def slices_arrived(kind):
        for d in (0, 1):
            arrived(slices.at[expert, 3 * kind + d], xy_recv.at[kind, d], d_to[d])
            arrived(slices.at[expert, 3 * kind + 2, :, pl.ds(d * (part_d // 2), part_d // 2)],
                    rf_recv.at[kind, d], d_to[d])

    og_pieces = 8
    og_rows = tokens // og_pieces

    def send_og(at):
        block = pl.ds(at * og_rows, og_rows)
        send(og_hbm.at[block], og_in.at[block], og_send.at[at], og_recv.at[at], p_to)

    ag_first()
    send_slices(x_hbm, 0)
    send_slices(rows_all, 1)
    send(routing_hbm, routing_in, rt_send, rt_recv, p_to)
    send(w_hbm.at[pl.ds(0, 2)], w_gu.at[core], w_send, w_recv, sib)
    gate_pre, up_pre = pre[:hid], pre[hid:]
    sigmoid = jax.nn.sigmoid(gate_pre)
    activated = gate_pre * sigmoid
    acts[0:hid, :] = (activated * up_pre).astype(BF16)
    act_g[...] = up_pre * sigmoid * (1.0 + gate_pre * (1.0 - sigmoid))
    act_u[...] = activated
    hidden_rows = pl.ds(0, hid)
    for d in (0, 1):
        send(acts.at[hidden_rows], acts_in.at[d, hidden_rows], h_send.at[d], h_recv.at[d], d_to[d])

    def relay_hidden():
        for d in (0, 1):
            arrived(acts_in.at[d, hidden_rows], h_recv.at[d], d_to[d])
            rows = pl.ds(d * (hid // 2), hid // 2)
            send(acts_in.at[d, rows], acts_in.at[2, rows], hf_send.at[d], hf_recv.at[d], d_to[d])

    for k in range(1, far):
        ag_step(k)
        if k == far - 2:
            relay_slices(0)
    if far < 3:
        relay_slices(0)
    relay_slices(1)
    for at in range(og_pieces // 2):
        send_og(at)
    ag_step(far)
    ag_finish()

    loads[3].wait()
    hidden_grad = into(lambda cols: w_d[:, cols], rows_all, hid)
    gate_grad = (hidden_grad * act_g[...]).astype(BF16)
    up_grad = (hidden_grad * act_u[...]).astype(BF16)
    acts[hid:2 * hid, :] = gate_grad
    acts[2 * hid:3 * hid, :] = up_grad
    both[core, 0:hid, :] = gate_grad
    both[core, hid:2 * hid, :] = up_grad
    send(acts.at[pl.ds(hid, 2 * hid)], both.at[core], t_send, t_recv, sib)
    for at in (0, 1):
        for d in (0, 1):
            m = at if d == 0 else 1 - at
            rows = pl.ds((1 + m) * hid, hid)
            send(acts.at[rows], acts_in.at[d, rows], g_send.at[d, m], g_recv.at[d, m], d_to[d])
    relay_hidden()
    for at in range(og_pieces // 2, og_pieces):
        send_og(at)
    slices_arrived(0)
    sl_first((0,))

    def relay_grads():
        for d in (0, 1):
            rows = pl.ds((1 + d) * hid, hid)
            arrived(acts_in.at[d, rows], g_recv.at[d, d], d_to[d])
            send(acts_in.at[d, rows], acts_in.at[2, rows], gf_send.at[d], gf_recv.at[d], d_to[d])

    arrived(both.at[1 - core], t_recv, sib)
    arrived(w_gu.at[1 - core], w_recv, sib)
    turned = jnp.transpose(both[...].reshape(4 * hid, rows_all.shape[0] * cap).astype(F32))
    wide[...] = turned.reshape(n_y, 2, cap, 4 * hid)
    mine = wide[:, core].reshape(n_y * cap, 4 * hid).astype(BF16)

    def partials(h):
        def body(at, carry):
            cols = pl.ds(pl.multiple_of(h * half + at * tile, tile), tile)
            weights = w_gu[:, :, :, cols].reshape(4 * hid, tile)
            part[:, :, cols] = jnp.dot(mine, weights, preferred_element_type=F32).reshape(
                n_y, cap, tile
            )
            return carry
        lax.fori_loop(0, half // tile, body, 0)

    def rs_send(d, k, h):
        cols = pl.ds(h * half, half)
        dest = (y + (k if d == 0 else -k) + n_y) % n_y
        value = part[dest, :, cols]
        if k < far and not (k == far - 1 and h != d):
            arrived(ring_in.at[d, k, :, cols], r_recv.at[d, k, h], y_to[d])
            value = value + ring_in[d, k, :, cols].astype(F32)
        ring_out[d, k - 1, :, cols] = value.astype(BF16)
        send(ring_out.at[d, k - 1, :, cols], ring_in.at[d, k - 1, :, cols],
             r_send.at[d, k - 1, h], r_recv.at[d, k - 1, h], y_to[d])

    def rs_step(k):
        for at in (0, 1):
            for d in (0, 1):
                rs_send(d, k, at if d == 0 else 1 - at)

    def add_grads(j, gate_up, down):
        own = j is None
        base = pl.multiple_of(dp * part_d, part_d)
        cell = part_d // 2
        for at in (0, 1):
            cols = pl.ds(at * cell, cell)
            here = pl.ds(pl.multiple_of(base + at * cell, cell), cell)
            if gate_up:
                left = acts[hid:3 * hid, :] if own else acts_in[j, hid:3 * hid, :]
                right = x[:, :, here] if own else slices[:, j, :, cols]
                value = jnp.dot(left, right.reshape(-1, cell), preferred_element_type=F32)
                acc_gu[:, cols] = value if own else acc_gu[:, cols] + value
            if down:
                left = acts[0:hid, :] if own else acts_in[j, 0:hid, :]
                right = rows_all[:, :, here] if own else slices[:, 3 + j, :, cols]
                value = jnp.dot(left, right.reshape(-1, cell), preferred_element_type=F32)
                acc_d[:, cols] = value if own else acc_d[:, cols] + value

    sl_step(1, (0,))
    partials(0)
    rs_send(0, far, 0)
    partials(1)
    rs_send(1, far, 1)
    rs_send(0, far - 1, 1)
    rs_send(1, far - 1, 0)
    sl_step(2, (0,))
    slices_arrived(1)
    sl_first((1,))
    for k in range(far - 1, 0, -1):
        if k == far - 1:
            rs_send(0, k, 0)
            rs_send(1, k, 1)
            add_grads(None, True, True)
        else:
            rs_step(k)
        step = far - k
        if step + 2 <= far:
            sl_step(step + 2, (0,))
        if step > 1:
            sl_step(step - 1, (1,))

    for h in (0, 1):
        cols = pl.ds(h * half, half)
        for d in (0, 1):
            if far > 1 or h == d:
                arrived(ring_in.at[d, 0, :, cols], r_recv.at[d, 0, h], y_to[d])
        total = part[y, :, cols] + (ring_in[0, 0, :, cols].astype(F32) + ring_in[1, 0, :, cols].astype(F32))
        final[:, cols] = (picked[:, cols] + total).astype(BF16)
        send(final.at[:, cols], final_in.at[:, cols], fin_send.at[h], fin_recv.at[h], p_to)

    relay_grads()
    for k in range(max(far - 1, 1), far + 1):
        sl_step(k, (1,))
    sl_finish()
    for d in (0, 1):
        rows = pl.ds(d * (hid // 2), hid // 2)
        arrived(acts_in.at[2, rows], hf_recv.at[d], d_to[d])
    for j in range(3):
        add_grads(j, False, True)
    for d in (0, 1):
        rows = pl.ds((2 - d) * hid, hid)
        arrived(acts_in.at[d, rows], g_recv.at[d, 1 - d], d_to[d])
        add_grads(d, True, False)

    arrived(routing_in, rt_recv, p_to)
    _, placed = one_hot(routing_in[...], cap)
    placed = placed.astype(BF16)
    named = lax.dot_general(
        placed, jnp.ones((cap, 128), BF16), TN, preferred_element_type=F32
    )[:, 0:1] > 0.5
    for at in range(og_pieces):
        block = pl.ds(at * og_rows, og_rows)
        arrived(og_in.at[block], og_recv.at[at], p_to)
    for h in (0, 1):
        arrived(final_in.at[:, pl.ds(h * half, half)], fin_recv.at[h], p_to)
    for at in range(4):
        cols = pl.ds(at * (width // 4), width // 4)
        value = lax.dot_general(placed, final_in[:, cols], TN, preferred_element_type=F32)
        passed_ref[:, cols] = jnp.where(named, value, og_in[:, cols].astype(F32)).astype(BF16)

    for d in (0, 1):
        rows = pl.ds((1 + d) * hid, hid)
        arrived(acts_in.at[2, rows], gf_recv.at[d], d_to[d])
    add_grads(2, True, False)
    grads_ref[0] = acc_gu[0:hid, :].astype(BF16)
    grads_ref[1] = acc_gu[hid:2 * hid, :].astype(BF16)
    grads_ref[2] = acc_d[...].astype(BF16)
    for copy in sent:
        copy.wait_send()


def shards(output_grads, gate_values, routing, saved_inputs, expert_weights):
    n_dp, n_pipe = lax.axis_size("dp"), lax.axis_size("pipe")
    devices = lax.axis_size("expert")
    n_y = devices // 2
    far = n_y // 2
    cap, width = saved_inputs.shape[4], saved_inputs.shape[5]
    tokens = output_grads.shape[2]
    hid = expert_weights.shape[2]
    rows = devices * cap
    part_d = width // n_dp
    DMA = pltpu.SemaphoreType.DMA
    V = pltpu.VMEM
    scratch = [
        V(routing.shape[:1:-1], jnp.int32),
        V(routing.shape[:1:-1], F32),
        V((tokens, width), BF16),
        V((devices, cap, width), BF16),
        V((2, 2, hid, width), BF16),
        V((hid, width), BF16),
        V((devices, cap, width), BF16),
        V((cap, width), F32),
        V((devices, 6, cap, part_d), BF16),
        V((2, 2, cap, part_d // 2), BF16),
        V((3 * hid, rows), BF16),
        V((3, 3 * hid, rows), BF16),
        V((2, 2 * hid, rows), BF16),
        V((n_y, 2, cap, 4 * hid), F32),
        V((n_y, cap, width), F32),
        V((2, far, cap, width), BF16),
        V((2, far, cap, width), BF16),
        V((tokens, width), BF16),
        V(routing.shape[:1:-1], jnp.int32),
        V((cap, width), BF16),
        V((cap, width), BF16),
        V((2 * hid, part_d), F32),
        V((hid, part_d), F32),
        V((hid, rows), F32),
        V((hid, rows), F32),
        DMA((6,)), DMA((8,)), DMA((8,)), DMA, DMA, DMA((2,)), DMA((2,)), DMA, DMA,
        DMA((2, far, 2)), DMA((2, far, 2)), DMA((n_y, 2)), DMA((n_y, 2)),
        DMA((2, far, 2)), DMA((2, far, 2)), DMA((n_y, 2)), DMA((n_y, 2)),
        DMA((2, 2)), DMA((2, 2)), DMA((2, 2)), DMA((2, 2)), DMA((2, 2)), DMA((2, 2)),
        DMA((2,)), DMA((2,)), DMA((2,)), DMA((2,)), DMA((2, 2)), DMA((2, 2)), DMA((2,)), DMA((2,)),
        DMA, DMA, DMA((2, far, 2)), DMA((2, far, 2)),
    ]
    vmem = pl.BlockSpec(memory_space=pltpu.VMEM)
    anywhere = pl.BlockSpec(memory_space=pltpu.HBM)
    passed, grads = pl.pallas_call(
        functools.partial(kernel, n_y, n_dp, n_pipe),
        out_shape=(
            pltpu.VMEM((tokens, width), BF16),
            pltpu.VMEM((3, hid, part_d), BF16),
        ),
        in_specs=[anywhere] * 5,
        out_specs=(vmem, vmem),
        scratch_shapes=scratch,
        compiler_params=pltpu.CompilerParams(
            collective_id=0, has_side_effects=True
        ),
        name="expert_backward",
    )(
        jnp.transpose(routing[0, 0]),
        jnp.transpose(gate_values[0, 0]),
        output_grads[0, 0],
        saved_inputs[0, 0, 0],
        expert_weights[0],
    )
    return passed[None, None], grads[None]


def solution(mesh):
    placed = (
        P("dp", "pipe", "expert", None),
        P("dp", "pipe", "expert", None),
        P("dp", "pipe", "expert", None),
        P("dp", "pipe", None, None, None, None),
        P("pipe", None, "expert", None),
    )
    return jax.shard_map(
        shards,
        mesh=mesh,
        in_specs=placed,
        out_specs=(P("dp", "pipe", "expert", None), P("pipe", None, "expert", "dp")),
        check_vma=False,
    )
```

```python
import functools

import jax
import jax.numpy as jnp
from jax import lax
from jax.experimental import pallas as pl
from jax.experimental.pallas import tpu as pltpu
from jax.sharding import PartitionSpec as P

MESH = pl.DeviceIdType.MESH
BF16 = jnp.bfloat16
F32 = jnp.float32
NT = (((1,), (1,)), ((), ()))
TN = (((0,), (0,)), ((), ()))


def one_hot(routing, capacity):
    tokens = routing.shape[1]
    hit = routing == 0
    member = jnp.max(jnp.where(hit, F32(1.0), F32(0.0)), axis=0, keepdims=True)
    before = lax.broadcasted_iota(jnp.int32, (tokens, tokens), 0) < lax.broadcasted_iota(
        jnp.int32, (tokens, tokens), 1
    )
    upper = jnp.where(before, F32(1.0), F32(0.0)).astype(BF16)
    rows = jnp.broadcast_to(member, (capacity, tokens))
    slot = jnp.dot(rows.astype(BF16), upper, preferred_element_type=F32)
    index = lax.broadcasted_iota(jnp.int32, (capacity, tokens), 0).astype(F32)
    return hit, jnp.where((slot == index) & (rows > 0.5), F32(1.0), F32(0.0))


def kernel(
    n_y, n_dp, n_pipe,
    routing_hbm, gates_hbm, og_hbm, x_hbm, w_hbm,
    passed_ref, grads_ref,
    routing_ref, gates_ref, og, x, w_gu, w_d, rows_all, picked, slices, relay, acts, acts_in, both, wide, part,
    ring_in, ring_out, og_in, routing_in, final, final_in, acc_gu, acc_d, act_g, act_u,
    load_sem, og_send, og_recv, rt_send, rt_recv, fin_send, fin_recv, w_send, w_recv,
    y_send, y_recv, ysib_send, ysib_recv, s_send, s_recv, ssib_send, ssib_recv,
    xy_send, xy_recv, rl_send, rl_recv, rf_send, rf_recv,
    h_send, h_recv, hf_send, hf_recv, g_send, g_recv, gf_send, gf_recv,
    t_send, t_recv, r_send, r_recv,
):
    dp = lax.axis_index("dp")
    pipe = lax.axis_index("pipe")
    expert = lax.axis_index("expert")
    y = expert // 2
    core = expert % 2
    far = n_y // 2
    cap, width = rows_all.shape[1], rows_all.shape[2]
    half = width // 2
    hid = w_d.shape[0]
    tokens = og.shape[0]
    part_d = width // n_dp
    tile = width // 8
    sib = {"expert": y * 2 + (1 - core)}
    y_to = ({"expert": ((y + 1) % n_y) * 2 + core}, {"expert": ((y + n_y - 1) % n_y) * 2 + core})
    d_to = ({"dp": (dp + 1) % n_dp}, {"dp": (dp + n_dp - 1) % n_dp})
    p_to = {"pipe": (pipe + n_pipe - 1) % n_pipe}
    p_from = {"pipe": (pipe + 1) % n_pipe}

    sent = []

    def send(src, dst, ssem, rsem, to):
        copy = pltpu.make_async_remote_copy(
            src_ref=src, dst_ref=dst, send_sem=ssem, recv_sem=rsem, device_id=to,
            device_id_type=MESH,
        )
        copy.start()
        sent.append(copy)

    def arrived(dst, rsem, to):
        pltpu.make_async_remote_copy(
            src_ref=dst, dst_ref=dst, send_sem=rsem, recv_sem=rsem, device_id=to,
            device_id_type=MESH,
        ).wait_recv()

    loads = [
        pltpu.make_async_copy(og_hbm, og, load_sem.at[0]),
        pltpu.make_async_copy(x_hbm, x, load_sem.at[1]),
        pltpu.make_async_copy(w_hbm.at[pl.ds(0, 2)], w_gu.at[core], load_sem.at[2]),
        pltpu.make_async_copy(w_hbm.at[2], w_d, load_sem.at[3]),
        pltpu.make_async_copy(routing_hbm, routing_ref, load_sem.at[4]),
        pltpu.make_async_copy(gates_hbm, gates_ref, load_sem.at[5]),
    ]
    barrier = pltpu.get_barrier_semaphore()
    peers = (sib, *y_to, *d_to, p_from)
    for peer in peers:
        pl.semaphore_signal(barrier, inc=1, device_id=peer, device_id_type=MESH)
    for at in (4, 5, 0, 1, 2, 3):
        loads[at].start()

    loads[4].wait()
    loads[5].wait()
    hit, chooser = one_hot(routing_ref[...], cap)
    share = jnp.sum(jnp.where(hit, gates_ref[...], F32(0.0)), axis=0, keepdims=True)
    weighting = jnp.sum(chooser * share, axis=1, keepdims=True)
    chooser = chooser.astype(BF16)
    loads[0].wait()
    for at in range(4):
        cols = pl.ds(at * (width // 4), width // 4)
        chosen = jnp.dot(chooser, og[:, cols], preferred_element_type=F32)
        picked[:, cols] = chosen
        rows_all[expert, :, cols] = (chosen * weighting).astype(BF16)
    pl.semaphore_wait(barrier, len(peers))

    def gather(piece, ring_send, ring_recv, sib_send, sib_recv):
        def owner(offset):
            return ((y + offset + n_y) % n_y) * 2 + core

        def first(pieces=(0, 1)):
            for at in range(len(pieces)):
                for d in (0, 1):
                    h = pieces[at if d == 0 else len(pieces) - 1 - at]
                    send(piece(expert, h), piece(expert, h), ring_send.at[d, 0, h],
                         ring_recv.at[d, 0, h], y_to[d])
            for h in pieces:
                send(piece(expert, h), piece(expert, h), sib_send.at[0, h], sib_recv.at[0, h], sib)

        def step(k, pieces=(0, 1)):
            for at in range(len(pieces)):
                for d in (0, 1):
                    h = pieces[at if d == 0 else len(pieces) - 1 - at]
                    if k == far and h != d:
                        continue
                    offset = -k if d == 0 else k
                    block = piece(owner(offset), h)
                    arrived(block, ring_recv.at[d, k - 1, h], y_to[d])
                    if k < far - 1 or (k == far - 1 and h == d):
                        send(block, block, ring_send.at[d, k, h], ring_recv.at[d, k, h], y_to[d])
                    slot = offset % n_y
                    send(block, block, sib_send.at[slot, h], sib_recv.at[slot, h], sib)

        def finish():
            for offset in range(n_y):
                for h in (0, 1):
                    other = ((y + offset) % n_y) * 2 + (1 - core)
                    arrived(piece(other, h), sib_recv.at[offset, h], sib)

        return first, step, finish

    ag_first, ag_step, ag_finish = gather(
        lambda e, h: rows_all.at[e, :, pl.ds(h * half, half)], y_send, y_recv, ysib_send, ysib_recv
    )
    sl_first, sl_step, sl_finish = gather(
        lambda e, h: slices.at[e, pl.ds(3 * h, 3)], s_send, s_recv, ssib_send, ssib_recv
    )

    def send_slices(src, kind):
        for d in (0, 1):
            peer = (dp + 1) % n_dp if d == 0 else (dp + n_dp - 1) % n_dp
            near = pl.ds(pl.multiple_of(peer * part_d, part_d), part_d)
            base = ((dp + 2) % n_dp) * part_d + d * (part_d // 2)
            beyond = pl.ds(pl.multiple_of(base, part_d // 2), part_d // 2)
            send(src.at[expert, :, beyond], relay.at[d, kind],
                 rl_send.at[kind, d], rl_recv.at[kind, d], d_to[d])
            send(src.at[expert, :, near], slices.at[expert, 3 * kind + d],
                 xy_send.at[kind, d], xy_recv.at[kind, d], d_to[d])

    def relay_slices(kind):
        for d in (0, 1):
            arrived(relay.at[d, kind], rl_recv.at[kind, d], d_to[d])
            send(relay.at[d, kind],
                 slices.at[expert, 3 * kind + 2, :, pl.ds(d * (part_d // 2), part_d // 2)],
                 rf_send.at[kind, d], rf_recv.at[kind, d], d_to[d])

    def slices_arrived(kind):
        for d in (0, 1):
            arrived(slices.at[expert, 3 * kind + d], xy_recv.at[kind, d], d_to[d])
            arrived(slices.at[expert, 3 * kind + 2, :, pl.ds(d * (part_d // 2), part_d // 2)],
                    rf_recv.at[kind, d], d_to[d])

    og_pieces = 8
    og_rows = tokens // og_pieces

    def send_og(at):
        block = pl.ds(at * og_rows, og_rows)
        send(og_hbm.at[block], og_in.at[block], og_send.at[at], og_recv.at[at], p_to)

    ag_first()
    send_slices(x_hbm, 0)
    send_slices(rows_all, 1)
    send(routing_hbm, routing_in, rt_send, rt_recv, p_to)
    send(w_hbm.at[pl.ds(0, 2)], w_gu.at[core], w_send, w_recv, sib)
    loads[1].wait()
    loads[2].wait()

    def into(weights, rows_ref, out_rows):
        def body(at, total):
            cols = pl.ds(pl.multiple_of(at * tile, tile), tile)
            rows = rows_ref[:, :, cols].reshape(-1, tile)
            return total + lax.dot_general(weights(cols), rows, NT, preferred_element_type=F32)
        rows = rows_ref.shape[0] * rows_ref.shape[1]
        return lax.fori_loop(0, width // tile, body, jnp.zeros((out_rows, rows), F32))

    pre = into(lambda cols: w_gu[core, :, :, cols].reshape(2 * hid, tile), x, 2 * hid)
    gate_pre, up_pre = pre[:hid], pre[hid:]
    sigmoid = jax.nn.sigmoid(gate_pre)
    activated = gate_pre * sigmoid
    acts[0:hid, :] = (activated * up_pre).astype(BF16)
    act_g[...] = up_pre * sigmoid * (1.0 + gate_pre * (1.0 - sigmoid))
    act_u[...] = activated
    hidden_rows = pl.ds(0, hid)
    for d in (0, 1):
        send(acts.at[hidden_rows], acts_in.at[d, hidden_rows], h_send.at[d], h_recv.at[d], d_to[d])

    def relay_hidden():
        for d in (0, 1):
            arrived(acts_in.at[d, hidden_rows], h_recv.at[d], d_to[d])
            rows = pl.ds(d * (hid // 2), hid // 2)
            send(acts_in.at[d, rows], acts_in.at[2, rows], hf_send.at[d], hf_recv.at[d], d_to[d])

    for k in range(1, far):
        ag_step(k)
        if k == far - 2:
            relay_slices(0)
    if far < 3:
        relay_slices(0)
    relay_slices(1)
    send_og(0)
    send_og(1)
    ag_step(far)
    ag_finish()

    loads[3].wait()
    hidden_grad = into(lambda cols: w_d[:, cols], rows_all, hid)
    gate_grad = (hidden_grad * act_g[...]).astype(BF16)
    up_grad = (hidden_grad * act_u[...]).astype(BF16)
    acts[hid:2 * hid, :] = gate_grad
    acts[2 * hid:3 * hid, :] = up_grad
    both[core, 0:hid, :] = gate_grad
    both[core, hid:2 * hid, :] = up_grad
    send(acts.at[pl.ds(hid, 2 * hid)], both.at[core], t_send, t_recv, sib)
    for at in (0, 1):
        for d in (0, 1):
            m = at if d == 0 else 1 - at
            rows = pl.ds((1 + m) * hid, hid)
            send(acts.at[rows], acts_in.at[d, rows], g_send.at[d, m], g_recv.at[d, m], d_to[d])
    relay_hidden()
    slices_arrived(0)
    sl_first((0,))

    def relay_grads():
        for d in (0, 1):
            rows = pl.ds((1 + d) * hid, hid)
            arrived(acts_in.at[d, rows], g_recv.at[d, d], d_to[d])
            send(acts_in.at[d, rows], acts_in.at[2, rows], gf_send.at[d], gf_recv.at[d], d_to[d])

    arrived(both.at[1 - core], t_recv, sib)
    arrived(w_gu.at[1 - core], w_recv, sib)
    turned = jnp.transpose(both[...].reshape(4 * hid, rows_all.shape[0] * cap).astype(F32))
    wide[...] = turned.reshape(n_y, 2, cap, 4 * hid)
    mine = wide[:, core].reshape(n_y * cap, 4 * hid).astype(BF16)

    def partials(h):
        def body(at, carry):
            cols = pl.ds(pl.multiple_of(h * half + at * tile, tile), tile)
            weights = w_gu[:, :, :, cols].reshape(4 * hid, tile)
            part[:, :, cols] = jnp.dot(mine, weights, preferred_element_type=F32).reshape(
                n_y, cap, tile
            )
            return carry
        lax.fori_loop(0, half // tile, body, 0)

    def rs_send(d, k, h):
        cols = pl.ds(h * half, half)
        dest = (y + (k if d == 0 else -k) + n_y) % n_y
        value = part[dest, :, cols]
        if k < far and not (k == far - 1 and h != d):
            arrived(ring_in.at[d, k, :, cols], r_recv.at[d, k, h], y_to[d])
            value = value + ring_in[d, k, :, cols].astype(F32)
        ring_out[d, k - 1, :, cols] = value.astype(BF16)
        send(ring_out.at[d, k - 1, :, cols], ring_in.at[d, k - 1, :, cols],
             r_send.at[d, k - 1, h], r_recv.at[d, k - 1, h], y_to[d])

    def rs_step(k):
        for at in (0, 1):
            for d in (0, 1):
                rs_send(d, k, at if d == 0 else 1 - at)

    def add_grads(j, gate_up, down):
        own = j is None
        base = pl.multiple_of(dp * part_d, part_d)
        cell = part_d // 2
        for at in (0, 1):
            cols = pl.ds(at * cell, cell)
            here = pl.ds(pl.multiple_of(base + at * cell, cell), cell)
            if gate_up:
                left = acts[hid:3 * hid, :] if own else acts_in[j, hid:3 * hid, :]
                right = x[:, :, here] if own else slices[:, j, :, cols]
                value = jnp.dot(left, right.reshape(-1, cell), preferred_element_type=F32)
                acc_gu[:, cols] = value if own else acc_gu[:, cols] + value
            if down:
                left = acts[0:hid, :] if own else acts_in[j, 0:hid, :]
                right = rows_all[:, :, here] if own else slices[:, 3 + j, :, cols]
                value = jnp.dot(left, right.reshape(-1, cell), preferred_element_type=F32)
                acc_d[:, cols] = value if own else acc_d[:, cols] + value

    partials(0)
    rs_send(0, far, 0)
    partials(1)
    rs_send(1, far, 1)
    rs_send(0, far - 1, 1)
    rs_send(1, far - 1, 0)
    sl_step(1, (0,))
    slices_arrived(1)
    sl_first((1,))
    for k in range(far - 1, 0, -1):
        if k == far - 1:
            rs_send(0, k, 0)
            rs_send(1, k, 1)
            add_grads(None, True, True)
        else:
            rs_step(k)
        if k < far - 1:
            sl_step(far - 1 - k, (1,))
        sl_step(far + 1 - k, (0,))
        if k == max(far - 2, 1):
            relay_grads()
            for at in range(2, og_pieces):
                send_og(at)

    for h in (0, 1):
        cols = pl.ds(h * half, half)
        for d in (0, 1):
            if far > 1 or h == d:
                arrived(ring_in.at[d, 0, :, cols], r_recv.at[d, 0, h], y_to[d])
        total = part[y, :, cols] + (ring_in[0, 0, :, cols].astype(F32) + ring_in[1, 0, :, cols].astype(F32))
        final[:, cols] = (picked[:, cols] + total).astype(BF16)
        send(final.at[:, cols], final_in.at[:, cols], fin_send.at[h], fin_recv.at[h], p_to)

    for k in range(far - 1, far + 1):
        sl_step(k, (1,))
    sl_finish()
    for d in (0, 1):
        rows = pl.ds(d * (hid // 2), hid // 2)
        arrived(acts_in.at[2, rows], hf_recv.at[d], d_to[d])
    for j in range(3):
        add_grads(j, False, True)
    for d in (0, 1):
        rows = pl.ds((2 - d) * hid, hid)
        arrived(acts_in.at[d, rows], g_recv.at[d, 1 - d], d_to[d])
        add_grads(d, True, False)

    for d in (0, 1):
        rows = pl.ds((1 + d) * hid, hid)
        arrived(acts_in.at[2, rows], gf_recv.at[d], d_to[d])
    add_grads(2, True, False)
    grads_ref[0] = acc_gu[0:hid, :].astype(BF16)
    grads_ref[1] = acc_gu[hid:2 * hid, :].astype(BF16)
    grads_ref[2] = acc_d[...].astype(BF16)

    arrived(routing_in, rt_recv, p_to)
    _, placed = one_hot(routing_in[...], cap)
    placed = placed.astype(BF16)
    named = lax.dot_general(
        placed, jnp.ones((cap, 128), BF16), TN, preferred_element_type=F32
    )[:, 0:1] > 0.5
    for at in range(og_pieces):
        block = pl.ds(at * og_rows, og_rows)
        arrived(og_in.at[block], og_recv.at[at], p_to)
    for h in (0, 1):
        arrived(final_in.at[:, pl.ds(h * half, half)], fin_recv.at[h], p_to)
    for at in range(4):
        cols = pl.ds(at * (width // 4), width // 4)
        value = lax.dot_general(placed, final_in[:, cols], TN, preferred_element_type=F32)
        passed_ref[:, cols] = jnp.where(named, value, og_in[:, cols].astype(F32)).astype(BF16)

    for copy in sent:
        copy.wait_send()


def shards(output_grads, gate_values, routing, saved_inputs, expert_weights):
    n_dp, n_pipe = lax.axis_size("dp"), lax.axis_size("pipe")
    devices = lax.axis_size("expert")
    n_y = devices // 2
    far = n_y // 2
    cap, width = saved_inputs.shape[4], saved_inputs.shape[5]
    tokens = output_grads.shape[2]
    hid = expert_weights.shape[2]
    rows = devices * cap
    part_d = width // n_dp
    DMA = pltpu.SemaphoreType.DMA
    V = pltpu.VMEM
    scratch = [
        V(routing.shape[:1:-1], jnp.int32),
        V(routing.shape[:1:-1], F32),
        V((tokens, width), BF16),
        V((devices, cap, width), BF16),
        V((2, 2, hid, width), BF16),
        V((hid, width), BF16),
        V((devices, cap, width), BF16),
        V((cap, width), F32),
        V((devices, 6, cap, part_d), BF16),
        V((2, 2, cap, part_d // 2), BF16),
        V((3 * hid, rows), BF16),
        V((3, 3 * hid, rows), BF16),
        V((2, 2 * hid, rows), BF16),
        V((n_y, 2, cap, 4 * hid), F32),
        V((n_y, cap, width), F32),
        V((2, far, cap, width), BF16),
        V((2, far, cap, width), BF16),
        V((tokens, width), BF16),
        V(routing.shape[:1:-1], jnp.int32),
        V((cap, width), BF16),
        V((cap, width), BF16),
        V((2 * hid, part_d), F32),
        V((hid, part_d), F32),
        V((hid, rows), F32),
        V((hid, rows), F32),
        DMA((6,)), DMA((8,)), DMA((8,)), DMA, DMA, DMA((2,)), DMA((2,)), DMA, DMA,
        DMA((2, far, 2)), DMA((2, far, 2)), DMA((n_y, 2)), DMA((n_y, 2)),
        DMA((2, far, 2)), DMA((2, far, 2)), DMA((n_y, 2)), DMA((n_y, 2)),
        DMA((2, 2)), DMA((2, 2)), DMA((2, 2)), DMA((2, 2)), DMA((2, 2)), DMA((2, 2)),
        DMA((2,)), DMA((2,)), DMA((2,)), DMA((2,)), DMA((2, 2)), DMA((2, 2)), DMA((2,)), DMA((2,)),
        DMA, DMA, DMA((2, far, 2)), DMA((2, far, 2)),
    ]
    vmem = pl.BlockSpec(memory_space=pltpu.VMEM)
    anywhere = pl.BlockSpec(memory_space=pltpu.HBM)
    passed, grads = pl.pallas_call(
        functools.partial(kernel, n_y, n_dp, n_pipe),
        out_shape=(
            pltpu.VMEM((tokens, width), BF16),
            pltpu.VMEM((3, hid, part_d), BF16),
        ),
        in_specs=[anywhere] * 5,
        out_specs=(vmem, vmem),
        scratch_shapes=scratch,
        compiler_params=pltpu.CompilerParams(
            collective_id=0, has_side_effects=True
        ),
        name="expert_backward",
    )(
        jnp.transpose(routing[0, 0]),
        jnp.transpose(gate_values[0, 0]),
        output_grads[0, 0],
        saved_inputs[0, 0, 0],
        expert_weights[0],
    )
    return passed[None, None], grads[None]


def solution(mesh):
    placed = (
        P("dp", "pipe", "expert", None),
        P("dp", "pipe", "expert", None),
        P("dp", "pipe", "expert", None),
        P("dp", "pipe", None, None, None, None),
        P("pipe", None, "expert", None),
    )
    return jax.shard_map(
        shards,
        mesh=mesh,
        in_specs=placed,
        out_specs=(P("dp", "pipe", "expert", None), P("pipe", None, "expert", "dp")),
        check_vma=False,
    )
```

```python
import functools

import jax
import jax.numpy as jnp
from jax import lax
from jax.experimental import pallas as pl
from jax.experimental.pallas import tpu as pltpu
from jax.sharding import PartitionSpec as P

MESH = pl.DeviceIdType.MESH
BF16 = jnp.bfloat16
F32 = jnp.float32
NT = (((1,), (1,)), ((), ()))
TN = (((0,), (0,)), ((), ()))


def one_hot(routing, capacity):
    tokens = routing.shape[1]
    hit = routing == 0
    member = jnp.max(jnp.where(hit, F32(1.0), F32(0.0)), axis=0, keepdims=True)
    before = lax.broadcasted_iota(jnp.int32, (tokens, tokens), 0) < lax.broadcasted_iota(
        jnp.int32, (tokens, tokens), 1
    )
    upper = jnp.where(before, F32(1.0), F32(0.0)).astype(BF16)
    rows = jnp.broadcast_to(member, (capacity, tokens))
    slot = jnp.dot(rows.astype(BF16), upper, preferred_element_type=F32)
    index = lax.broadcasted_iota(jnp.int32, (capacity, tokens), 0).astype(F32)
    return hit, jnp.where((slot == index) & (rows > 0.5), F32(1.0), F32(0.0))


def write_out(passed_ref, grads_ref, passed_hbm, grads_hbm, sems):
    half = passed_ref.shape[0] // 2
    copies = [
        pltpu.make_async_copy(passed_ref.at[pl.ds(0, half)], passed_hbm.at[pl.ds(0, half)], sems.at[0]),
        pltpu.make_async_copy(passed_ref.at[pl.ds(half, half)], passed_hbm.at[pl.ds(half, half)], sems.at[1]),
        pltpu.make_async_copy(grads_ref, grads_hbm, sems.at[2]),
    ]
    for copy in copies:
        copy.start()
    for copy in copies:
        copy.wait()


def kernel(
    n_y, n_dp, n_pipe,
    routing_hbm, gates_hbm, og_hbm, x_hbm, w_hbm,
    passed_ref, grads_ref,
    routing_ref, gates_ref, og, x, w_gu, w_d, rows_all, picked, slices, relay, acts, acts_in, both, wide, part,
    ring_in, ring_out, og_in, routing_in, final, final_in, acc_gu, acc_d, act_g, act_u,
    load_sem, og_send, og_recv, rt_send, rt_recv, fin_send, fin_recv, w_send, w_recv,
    y_send, y_recv, ysib_send, ysib_recv, s_send, s_recv, ssib_send, ssib_recv,
    xy_send, xy_recv, rl_send, rl_recv, rf_send, rf_recv,
    h_send, h_recv, hf_send, hf_recv, g_send, g_recv, gf_send, gf_recv,
    t_send, t_recv, r_send, r_recv,
):
    dp = lax.axis_index("dp")
    pipe = lax.axis_index("pipe")
    expert = lax.axis_index("expert")
    y = expert // 2
    core = expert % 2
    far = n_y // 2
    cap, width = rows_all.shape[1], rows_all.shape[2]
    half = width // 2
    hid = w_d.shape[0]
    tokens = og.shape[0]
    part_d = width // n_dp
    tile = width // 8
    sib = {"expert": y * 2 + (1 - core)}
    y_to = ({"expert": ((y + 1) % n_y) * 2 + core}, {"expert": ((y + n_y - 1) % n_y) * 2 + core})
    d_to = ({"dp": (dp + 1) % n_dp}, {"dp": (dp + n_dp - 1) % n_dp})
    p_to = {"pipe": (pipe + n_pipe - 1) % n_pipe}
    p_from = {"pipe": (pipe + 1) % n_pipe}

    sent = []

    def send(src, dst, ssem, rsem, to):
        copy = pltpu.make_async_remote_copy(
            src_ref=src, dst_ref=dst, send_sem=ssem, recv_sem=rsem, device_id=to,
            device_id_type=MESH,
        )
        copy.start()
        sent.append(copy)

    def arrived(dst, rsem, to):
        pltpu.make_async_remote_copy(
            src_ref=dst, dst_ref=dst, send_sem=rsem, recv_sem=rsem, device_id=to,
            device_id_type=MESH,
        ).wait_recv()

    loads = [
        pltpu.make_async_copy(og_hbm, og, load_sem.at[0]),
        pltpu.make_async_copy(x_hbm, x, load_sem.at[1]),
        pltpu.make_async_copy(w_hbm.at[pl.ds(0, 2)], w_gu.at[core], load_sem.at[2]),
        pltpu.make_async_copy(w_hbm.at[2], w_d, load_sem.at[3]),
        pltpu.make_async_copy(routing_hbm, routing_ref, load_sem.at[4]),
        pltpu.make_async_copy(gates_hbm, gates_ref, load_sem.at[5]),
    ]
    barrier = pltpu.get_barrier_semaphore()
    peers = (sib, *y_to, *d_to, p_from)
    for peer in peers:
        pl.semaphore_signal(barrier, inc=1, device_id=peer, device_id_type=MESH)
    for at in (4, 5, 0, 1, 2, 3):
        loads[at].start()

    loads[4].wait()
    loads[5].wait()
    hit, chooser = one_hot(routing_ref[...], cap)
    share = jnp.sum(jnp.where(hit, gates_ref[...], F32(0.0)), axis=0, keepdims=True)
    weighting = jnp.sum(chooser * share, axis=1, keepdims=True)
    chooser = chooser.astype(BF16)
    loads[0].wait()
    for at in range(4):
        cols = pl.ds(at * (width // 4), width // 4)
        chosen = jnp.dot(chooser, og[:, cols], preferred_element_type=F32)
        picked[:, cols] = chosen
        rows_all[expert, :, cols] = (chosen * weighting).astype(BF16)
    pl.semaphore_wait(barrier, len(peers))

    def gather(piece, ring_send, ring_recv, sib_send, sib_recv):
        def owner(offset):
            return ((y + offset + n_y) % n_y) * 2 + core

        def first(pieces=(0, 1)):
            for at in range(len(pieces)):
                for d in (0, 1):
                    h = pieces[at if d == 0 else len(pieces) - 1 - at]
                    send(piece(expert, h), piece(expert, h), ring_send.at[d, 0, h],
                         ring_recv.at[d, 0, h], y_to[d])
            for h in pieces:
                send(piece(expert, h), piece(expert, h), sib_send.at[0, h], sib_recv.at[0, h], sib)

        def step(k, pieces=(0, 1)):
            for at in range(len(pieces)):
                for d in (0, 1):
                    h = pieces[at if d == 0 else len(pieces) - 1 - at]
                    if k == far and h != d:
                        continue
                    offset = -k if d == 0 else k
                    block = piece(owner(offset), h)
                    arrived(block, ring_recv.at[d, k - 1, h], y_to[d])
                    if k < far - 1 or (k == far - 1 and h == d):
                        send(block, block, ring_send.at[d, k, h], ring_recv.at[d, k, h], y_to[d])
                    slot = offset % n_y
                    send(block, block, sib_send.at[slot, h], sib_recv.at[slot, h], sib)

        def finish():
            for offset in range(n_y):
                for h in (0, 1):
                    other = ((y + offset) % n_y) * 2 + (1 - core)
                    arrived(piece(other, h), sib_recv.at[offset, h], sib)

        return first, step, finish

    ag_first, ag_step, ag_finish = gather(
        lambda e, h: rows_all.at[e, :, pl.ds(h * half, half)], y_send, y_recv, ysib_send, ysib_recv
    )
    sl_first, sl_step, sl_finish = gather(
        lambda e, h: slices.at[e, pl.ds(3 * h, 3)], s_send, s_recv, ssib_send, ssib_recv
    )

    def send_slices(src, kind):
        for d in (0, 1):
            peer = (dp + 1) % n_dp if d == 0 else (dp + n_dp - 1) % n_dp
            near = pl.ds(pl.multiple_of(peer * part_d, part_d), part_d)
            base = ((dp + 2) % n_dp) * part_d + d * (part_d // 2)
            beyond = pl.ds(pl.multiple_of(base, part_d // 2), part_d // 2)
            send(src.at[expert, :, beyond], relay.at[d, kind],
                 rl_send.at[kind, d], rl_recv.at[kind, d], d_to[d])
            send(src.at[expert, :, near], slices.at[expert, 3 * kind + d],
                 xy_send.at[kind, d], xy_recv.at[kind, d], d_to[d])

    def relay_slices(kind):
        for d in (0, 1):
            arrived(relay.at[d, kind], rl_recv.at[kind, d], d_to[d])
            send(relay.at[d, kind],
                 slices.at[expert, 3 * kind + 2, :, pl.ds(d * (part_d // 2), part_d // 2)],
                 rf_send.at[kind, d], rf_recv.at[kind, d], d_to[d])

    def slices_arrived(kind):
        for d in (0, 1):
            arrived(slices.at[expert, 3 * kind + d], xy_recv.at[kind, d], d_to[d])
            arrived(slices.at[expert, 3 * kind + 2, :, pl.ds(d * (part_d // 2), part_d // 2)],
                    rf_recv.at[kind, d], d_to[d])

    og_pieces = 8
    og_rows = tokens // og_pieces

    def send_og(at):
        block = pl.ds(at * og_rows, og_rows)
        send(og_hbm.at[block], og_in.at[block], og_send.at[at], og_recv.at[at], p_to)

    ag_first()
    send_slices(x_hbm, 0)
    send_slices(rows_all, 1)
    send(routing_hbm, routing_in, rt_send, rt_recv, p_to)
    send(w_hbm.at[pl.ds(0, 2)], w_gu.at[core], w_send, w_recv, sib)
    loads[1].wait()
    loads[2].wait()

    def into(weights, rows_ref, out_rows):
        def body(at, total):
            cols = pl.ds(pl.multiple_of(at * tile, tile), tile)
            rows = rows_ref[:, :, cols].reshape(-1, tile)
            return total + lax.dot_general(weights(cols), rows, NT, preferred_element_type=F32)
        rows = rows_ref.shape[0] * rows_ref.shape[1]
        return lax.fori_loop(0, width // tile, body, jnp.zeros((out_rows, rows), F32))

    pre = into(lambda cols: w_gu[core, :, :, cols].reshape(2 * hid, tile), x, 2 * hid)
    gate_pre, up_pre = pre[:hid], pre[hid:]
    sigmoid = jax.nn.sigmoid(gate_pre)
    activated = gate_pre * sigmoid
    acts[0:hid, :] = (activated * up_pre).astype(BF16)
    act_g[...] = up_pre * sigmoid * (1.0 + gate_pre * (1.0 - sigmoid))
    act_u[...] = activated
    hidden_rows = pl.ds(0, hid)
    for d in (0, 1):
        send(acts.at[hidden_rows], acts_in.at[d, hidden_rows], h_send.at[d], h_recv.at[d], d_to[d])

    def relay_hidden():
        for d in (0, 1):
            arrived(acts_in.at[d, hidden_rows], h_recv.at[d], d_to[d])
            rows = pl.ds(d * (hid // 2), hid // 2)
            send(acts_in.at[d, rows], acts_in.at[2, rows], hf_send.at[d], hf_recv.at[d], d_to[d])

    for k in range(1, far):
        ag_step(k)
        if k == far - 2:
            relay_slices(0)
    if far < 3:
        relay_slices(0)
    relay_slices(1)
    send_og(0)
    send_og(1)
    ag_step(far)
    ag_finish()

    loads[3].wait()
    hidden_grad = into(lambda cols: w_d[:, cols], rows_all, hid)
    gate_grad = (hidden_grad * act_g[...]).astype(BF16)
    up_grad = (hidden_grad * act_u[...]).astype(BF16)
    acts[hid:2 * hid, :] = gate_grad
    acts[2 * hid:3 * hid, :] = up_grad
    both[core, 0:hid, :] = gate_grad
    both[core, hid:2 * hid, :] = up_grad
    send(acts.at[pl.ds(hid, 2 * hid)], both.at[core], t_send, t_recv, sib)
    for at in (0, 1):
        for d in (0, 1):
            m = at if d == 0 else 1 - at
            rows = pl.ds((1 + m) * hid, hid)
            send(acts.at[rows], acts_in.at[d, rows], g_send.at[d, m], g_recv.at[d, m], d_to[d])
    relay_hidden()
    slices_arrived(0)
    sl_first((0,))

    def relay_grads():
        for d in (0, 1):
            rows = pl.ds((1 + d) * hid, hid)
            arrived(acts_in.at[d, rows], g_recv.at[d, d], d_to[d])
            send(acts_in.at[d, rows], acts_in.at[2, rows], gf_send.at[d], gf_recv.at[d], d_to[d])

    arrived(both.at[1 - core], t_recv, sib)
    arrived(w_gu.at[1 - core], w_recv, sib)
    turned = jnp.transpose(both[...].reshape(4 * hid, rows_all.shape[0] * cap).astype(F32))
    wide[...] = turned.reshape(n_y, 2, cap, 4 * hid)
    mine = wide[:, core].reshape(n_y * cap, 4 * hid).astype(BF16)

    def partials(h):
        def body(at, carry):
            cols = pl.ds(pl.multiple_of(h * half + at * tile, tile), tile)
            weights = w_gu[:, :, :, cols].reshape(4 * hid, tile)
            part[:, :, cols] = jnp.dot(mine, weights, preferred_element_type=F32).reshape(
                n_y, cap, tile
            )
            return carry
        lax.fori_loop(0, half // tile, body, 0)

    def rs_send(d, k, h):
        cols = pl.ds(h * half, half)
        dest = (y + (k if d == 0 else -k) + n_y) % n_y
        value = part[dest, :, cols]
        if k < far and not (k == far - 1 and h != d):
            arrived(ring_in.at[d, k, :, cols], r_recv.at[d, k, h], y_to[d])
            value = value + ring_in[d, k, :, cols].astype(F32)
        ring_out[d, k - 1, :, cols] = value.astype(BF16)
        send(ring_out.at[d, k - 1, :, cols], ring_in.at[d, k - 1, :, cols],
             r_send.at[d, k - 1, h], r_recv.at[d, k - 1, h], y_to[d])

    def rs_step(k):
        for at in (0, 1):
            for d in (0, 1):
                rs_send(d, k, at if d == 0 else 1 - at)

    def add_grads(j, gate_up, down):
        own = j is None
        base = pl.multiple_of(dp * part_d, part_d)
        cell = part_d // 2
        for at in (0, 1):
            cols = pl.ds(at * cell, cell)
            here = pl.ds(pl.multiple_of(base + at * cell, cell), cell)
            if gate_up:
                left = acts[hid:3 * hid, :] if own else acts_in[j, hid:3 * hid, :]
                right = x[:, :, here] if own else slices[:, j, :, cols]
                value = jnp.dot(left, right.reshape(-1, cell), preferred_element_type=F32)
                acc_gu[:, cols] = value if own else acc_gu[:, cols] + value
            if down:
                left = acts[0:hid, :] if own else acts_in[j, 0:hid, :]
                right = rows_all[:, :, here] if own else slices[:, 3 + j, :, cols]
                value = jnp.dot(left, right.reshape(-1, cell), preferred_element_type=F32)
                acc_d[:, cols] = value if own else acc_d[:, cols] + value

    partials(0)
    rs_send(0, far, 0)
    partials(1)
    rs_send(1, far, 1)
    rs_send(0, far - 1, 1)
    rs_send(1, far - 1, 0)
    sl_step(1, (0,))
    slices_arrived(1)
    sl_first((1,))
    for k in range(far - 1, 0, -1):
        if k == far - 1:
            rs_send(0, k, 0)
            rs_send(1, k, 1)
            add_grads(None, True, True)
        else:
            rs_step(k)
        if k < far - 1:
            sl_step(far - 1 - k, (1,))
        sl_step(far + 1 - k, (0,))
        if k == max(far - 2, 1):
            relay_grads()
            send_og(2)
            send_og(3)
        if k == 1:
            send_og(4)
            send_og(5)

    for h in (0, 1):
        cols = pl.ds(h * half, half)
        for d in (0, 1):
            if far > 1 or h == d:
                arrived(ring_in.at[d, 0, :, cols], r_recv.at[d, 0, h], y_to[d])
        total = part[y, :, cols] + (ring_in[0, 0, :, cols].astype(F32) + ring_in[1, 0, :, cols].astype(F32))
        final[:, cols] = (picked[:, cols] + total).astype(BF16)
        send(final.at[:, cols], final_in.at[:, cols], fin_send.at[h], fin_recv.at[h], p_to)

    send_og(6)
    send_og(7)
    for k in range(far - 1, far + 1):
        sl_step(k, (1,))
    sl_finish()
    for d in (0, 1):
        rows = pl.ds(d * (hid // 2), hid // 2)
        arrived(acts_in.at[2, rows], hf_recv.at[d], d_to[d])
    for j in range(3):
        add_grads(j, False, True)
    for d in (0, 1):
        rows = pl.ds((2 - d) * hid, hid)
        arrived(acts_in.at[d, rows], g_recv.at[d, 1 - d], d_to[d])
        add_grads(d, True, False)

    for d in (0, 1):
        rows = pl.ds((1 + d) * hid, hid)
        arrived(acts_in.at[2, rows], gf_recv.at[d], d_to[d])
    add_grads(2, True, False)
    grads_ref[0] = acc_gu[0:hid, :].astype(BF16)
    grads_ref[1] = acc_gu[hid:2 * hid, :].astype(BF16)
    grads_ref[2] = acc_d[...].astype(BF16)

    arrived(routing_in, rt_recv, p_to)
    _, placed = one_hot(routing_in[...], cap)
    placed = placed.astype(BF16)
    named = lax.dot_general(
        placed, jnp.ones((cap, 128), BF16), TN, preferred_element_type=F32
    )[:, 0:1] > 0.5
    for at in range(og_pieces):
        block = pl.ds(at * og_rows, og_rows)
        arrived(og_in.at[block], og_recv.at[at], p_to)
    for h in (0, 1):
        arrived(final_in.at[:, pl.ds(h * half, half)], fin_recv.at[h], p_to)
    for at in range(4):
        cols = pl.ds(at * (width // 4), width // 4)
        value = lax.dot_general(placed, final_in[:, cols], TN, preferred_element_type=F32)
        passed_ref[:, cols] = jnp.where(named, value, og_in[:, cols].astype(F32)).astype(BF16)

    for copy in sent:
        copy.wait_send()


def shards(output_grads, gate_values, routing, saved_inputs, expert_weights):
    n_dp, n_pipe = lax.axis_size("dp"), lax.axis_size("pipe")
    devices = lax.axis_size("expert")
    n_y = devices // 2
    far = n_y // 2
    cap, width = saved_inputs.shape[4], saved_inputs.shape[5]
    tokens = output_grads.shape[2]
    hid = expert_weights.shape[2]
    rows = devices * cap
    part_d = width // n_dp
    DMA = pltpu.SemaphoreType.DMA
    V = pltpu.VMEM
    scratch = [
        V(routing.shape[:1:-1], jnp.int32),
        V(routing.shape[:1:-1], F32),
        V((tokens, width), BF16),
        V((devices, cap, width), BF16),
        V((2, 2, hid, width), BF16),
        V((hid, width), BF16),
        V((devices, cap, width), BF16),
        V((cap, width), F32),
        V((devices, 6, cap, part_d), BF16),
        V((2, 2, cap, part_d // 2), BF16),
        V((3 * hid, rows), BF16),
        V((3, 3 * hid, rows), BF16),
        V((2, 2 * hid, rows), BF16),
        V((n_y, 2, cap, 4 * hid), F32),
        V((n_y, cap, width), F32),
        V((2, far, cap, width), BF16),
        V((2, far, cap, width), BF16),
        V((tokens, width), BF16),
        V(routing.shape[:1:-1], jnp.int32),
        V((cap, width), BF16),
        V((cap, width), BF16),
        V((2 * hid, part_d), F32),
        V((hid, part_d), F32),
        V((hid, rows), F32),
        V((hid, rows), F32),
        DMA((6,)), DMA((8,)), DMA((8,)), DMA, DMA, DMA((2,)), DMA((2,)), DMA, DMA,
        DMA((2, far, 2)), DMA((2, far, 2)), DMA((n_y, 2)), DMA((n_y, 2)),
        DMA((2, far, 2)), DMA((2, far, 2)), DMA((n_y, 2)), DMA((n_y, 2)),
        DMA((2, 2)), DMA((2, 2)), DMA((2, 2)), DMA((2, 2)), DMA((2, 2)), DMA((2, 2)),
        DMA((2,)), DMA((2,)), DMA((2,)), DMA((2,)), DMA((2, 2)), DMA((2, 2)), DMA((2,)), DMA((2,)),
        DMA, DMA, DMA((2, far, 2)), DMA((2, far, 2)),
    ]
    vmem = pl.BlockSpec(memory_space=pltpu.VMEM)
    anywhere = pl.BlockSpec(memory_space=pltpu.HBM)
    passed, grads = pl.pallas_call(
        functools.partial(kernel, n_y, n_dp, n_pipe),
        out_shape=(
            pltpu.VMEM((tokens, width), BF16),
            pltpu.VMEM((3, hid, part_d), BF16),
        ),
        in_specs=[anywhere] * 5,
        out_specs=(vmem, vmem),
        scratch_shapes=scratch,
        compiler_params=pltpu.CompilerParams(
            collective_id=0, has_side_effects=True
        ),
        name="expert_backward",
    )(
        jnp.transpose(routing[0, 0]),
        jnp.transpose(gate_values[0, 0]),
        output_grads[0, 0],
        saved_inputs[0, 0, 0],
        expert_weights[0],
    )
    passed, grads = pl.pallas_call(
        write_out,
        out_shape=(
            jax.ShapeDtypeStruct((tokens, width), BF16),
            jax.ShapeDtypeStruct((3, hid, part_d), BF16),
        ),
        in_specs=[vmem, vmem],
        out_specs=(anywhere, anywhere),
        scratch_shapes=[DMA((3,))],
        compiler_params=pltpu.CompilerParams(vmem_limit_bytes=8 << 20),
        name="write_out",
    )(passed, grads)
    return passed[None, None], grads[None]


def solution(mesh):
    placed = (
        P("dp", "pipe", "expert", None),
        P("dp", "pipe", "expert", None),
        P("dp", "pipe", "expert", None),
        P("dp", "pipe", None, None, None, None),
        P("pipe", None, "expert", None),
    )
    return jax.shard_map(
        shards,
        mesh=mesh,
        in_specs=placed,
        out_specs=(P("dp", "pipe", "expert", None), P("pipe", None, "expert", "dp")),
        check_vma=False,
    )
```
